32 devices in a mesh: line: 8 (over z, x), span: 4 (over y, core).
Axes of the slice: x: 2, y: 2, z: 4, core: 2. Of those that a mesh axis runs over, the one named last changes fastest.
Arguments:
- forcing: float32 [32, 256, 256], P('span', 'line'), may hold values from -1 to 1
- blocks: float32 [256, 256, 256], P(('line', 'span')), may hold values from -1 to 1
- upstream: float32 [256, 256], P(('line', 'span')), may hold values from -2 to 0
Outputs:
- solution: float32 [32, 256, 256], P('span', 'line')
The draws below stay inside these ranges and needn't reach their ends.
All inputs are finite; a program needn't handle non-finite values.
Results may differ from the reference program's by a relative error of at most 0.0003.
Values sent between devices are 32-bit elements; how exact they have to be, the bound alone decides.
A program may use at most 192 MiB of HBM per device.

```python
import math
import jax
import jax.numpy as jnp
from jax import lax

LEVELS = 256
LINES = 32
CELLS = 256


def coefficients(key):
    share = 5
    slow = jax.random.randint(jax.random.fold_in(key, 1), (LEVELS,), 0, 10) < share
    diag_part = jax.random.uniform(jax.random.fold_in(key, 2), (CELLS, LEVELS), jnp.float32, 0.5, 1.0)
    slow_base = jnp.exp(jax.random.uniform(jax.random.fold_in(key, 3), (LEVELS,), jnp.float32, math.log(0.4), math.log(1.2))) / CELLS
    fast_base = jnp.exp(jax.random.uniform(jax.random.fold_in(key, 4), (LEVELS,), jnp.float32, math.log(1.0 / 300.0), math.log(1.0 / 30.0)))
    base_rate = jnp.where(slow, slow_base, fast_base)
    where_cell = jnp.arange(CELLS).astype(jnp.float32) / CELLS
    phase = jax.random.uniform(jax.random.fold_in(key, 5), (), jnp.float32, 0.0, 2.0 * math.pi)
    region = 1.0 + 0.4 * jnp.sin(2.0 * math.pi * 3.0 * where_cell + phase)
    rough = jax.random.uniform(jax.random.fold_in(key, 6), (CELLS, LEVELS), jnp.float32, 0.7, 1.4)
    retain = 1.0 - base_rate[None, :] * region[:, None] * rough
    spots = jax.random.randint(jax.random.fold_in(key, 7), (3,), 0, CELLS)
    depth = jax.random.uniform(jax.random.fold_in(key, 8), (3,), jnp.float32, 0.5, 0.8)
    hits = jnp.where(jnp.arange(CELLS)[:, None] == spots[None, :], depth[None, :], 1.0)
    retain = retain * jnp.prod(hits, axis=1)[:, None]
    off_diag = ~jnp.eye(LEVELS, dtype=bool)
    same_class = (slow[:, None] == slow[None, :]) & off_diag
    cross_pick = jax.random.randint(jax.random.fold_in(key, 10), (CELLS, LEVELS, LEVELS), 0, 10) == 0
    unit = 0.2 / math.sqrt(LEVELS / 2)
    entry_scale = jnp.where(same_class[None, :, :], unit, jnp.where(cross_pick & off_diag[None, :, :], 0.3 * unit, 0.0))
    noise = jnp.clip(jax.random.normal(jax.random.fold_in(key, 9), (CELLS, LEVELS, LEVELS), jnp.float32), -4.0, 4.0)
    off_part = noise * entry_scale
    whole = off_part + jnp.eye(LEVELS, dtype=jnp.float32)[None, :, :] * diag_part[:, :, None]
    energy = diag_part * diag_part + jnp.sum(off_part * off_part, axis=2)
    coupling = -retain / jnp.sqrt(energy)
    return (whole, coupling)


def draw_blocks(key, part):
    whole, coupling = coefficients(key)
    return whole.astype(jnp.float32)


def draw_upstream(key, part):
    whole, coupling = coefficients(key)
    return coupling.astype(jnp.float32)


def draw_forcing(key, part):
    values = 0.1 * jnp.clip(jax.random.normal(jax.random.fold_in(key, 12), (LINES, CELLS, LEVELS), jnp.float32), -6.0, 6.0)
    return values.astype(jnp.float32)


def setup_inputs(seed: int = 0) -> dict:
    key_list = jax.random.split(jax.random.key(seed), 4)
    return {
        "forcing": draw_forcing(jax.random.fold_in(key_list[3], 71), 0),
        "blocks": draw_blocks(jax.random.fold_in(key_list[3], 71), 0),
        "upstream": draw_upstream(jax.random.fold_in(key_list[3], 71), 0),
    }


def reference(forcing, blocks, upstream):
    initial = jnp.zeros((forcing.shape[0], forcing.shape[2]), jnp.float32)

    def advance(carried, cell_items):
        cell_forcing, cell_block, cell_upstream = cell_items
        updated = jnp.dot(cell_forcing - cell_upstream[None, :] * carried, cell_block,
                          precision=lax.Precision.HIGHEST, preferred_element_type=jnp.float32)
        return updated, updated

    _, history = lax.scan(advance, initial, (jnp.moveaxis(forcing, 1, 0), blocks, upstream))
    return jnp.moveaxis(history, 0, 1)
```

```python
import functools

import jax
import jax.numpy as jnp
from jax import lax
from jax.experimental import pallas as pl
from jax.experimental.pallas import tpu as pltpu
from jax.sharding import PartitionSpec as P

MESH = pl.DeviceIdType.MESH
RUN = 2


def split(value):
    high = value.astype(jnp.bfloat16)
    return high, (value - high.astype(jnp.float32)).astype(jnp.bfloat16)


def dot(a, b):
    return jnp.dot(a, b, preferred_element_type=jnp.float32)


def times(value, high, low):
    rows = value.shape[0]
    value_high, value_low = split(value)
    both = dot(jnp.concatenate([value_high, value_low], axis=0), high)
    return both[:rows] + both[rows:] + dot(value_high, low)


def kernel(
    lines_count,
    span_count,
    forcing,
    blocks,
    upstream,
    out,
    cells_in,
    held,
    block_high,
    block_low,
    map_high,
    map_low,
    trial,
    pair_maps,
    pair_states,
    maps,
    states,
    ahead_maps,
    ahead_states,
    entering,
    leaving,
    solved,
    block_sem,
    force_send,
    force_recv,
    pair_send,
    pair_recv,
    map_send,
    map_recv,
    pass_send,
    pass_recv,
    state_send,
    state_recv,
    chain_send,
    chain_recv,
    out_sem,
    out_send,
    out_recv,
):
    line, span = lax.axis_index("line"), lax.axis_index("span")
    cells, levels = upstream.shape
    own_lines = forcing.shape[0]
    half_span = span_count // 2
    pairs = RUN * half_span
    runs = lines_count // RUN
    run, place = line // RUN, line % RUN
    row, core = span // 2, span % 2
    pair = place * half_span + row
    partner = (line, row * 2 + (1 - core))
    half = levels // 2
    mine = pl.ds(pl.multiple_of(core * half, half), half)

    shifts = [(a, b) for a in range(RUN) for b in range(half_span) if (a, b) != (0, 0)]

    def peer(shift, sign):
        other_place = (place + sign * shift[0] + RUN) % RUN
        other_row = (row + sign * shift[1] + half_span) % half_span
        return (run * RUN + other_place, other_row * 2 + core), other_place * half_span + other_row

    def remote(source, target, send, recv, device):
        return pltpu.make_async_remote_copy(
            src_ref=source,
            dst_ref=target,
            send_sem=send,
            recv_sem=recv,
            device_id=device,
            device_id_type=MESH,
        )

    loads = [
        pltpu.make_async_copy(blocks.at[cell], held.at[cell], block_sem.at[cell])
        for cell in range(cells)
    ]
    for load in loads:
        load.start()

    barrier = pltpu.get_barrier_semaphore()
    greeted = 0
    for step in range(1, span_count):
        pl.semaphore_signal(
            barrier, inc=1, device_id=(line, (span + step) % span_count), device_id_type=MESH
        )
        greeted += 1
    for shift in shifts:
        if shift[0] != 0:
            pl.semaphore_signal(barrier, inc=1, device_id=peer(shift, 1)[0], device_id_type=MESH)
            greeted += 1
    first, last = run == 0, run == runs - 1

    @pl.when(jnp.logical_not(first))
    def _():
        pl.semaphore_signal(barrier, inc=1, device_id=(line - RUN, span), device_id_type=MESH)

    @pl.when(jnp.logical_not(last))
    def _():
        pl.semaphore_signal(barrier, inc=1, device_id=(line + RUN, span), device_id_type=MESH)

    chained = jnp.where(first, 0, 1) + jnp.where(last, 0, 1)
    pl.semaphore_wait(barrier, greeted + chained)

    own_rows = pl.ds(pl.multiple_of(span * own_lines, own_lines), own_lines)
    own_cells = pl.ds(pl.multiple_of(span * cells, cells), cells)
    force_copies = []
    for step in range(1, span_count):
        other = (span + step) % span_count
        other_cells = pl.ds(pl.multiple_of(other * cells, cells), cells)
        copy = remote(
            forcing.at[:, other_cells, :],
            cells_in.at[own_rows],
            force_send.at[step],
            force_recv.at[step],
            (line, other),
        )
        copy.start()
        force_copies.append(copy)
    cells_in[own_rows] = forcing[:, own_cells, :]

    factors = -upstream[...]
    for cell in range(cells):
        loads[cell].wait()
        value = held[cell]
        high, low = split(value)
        block_high[cell] = high
        block_low[cell] = low
        if cell == 0:
            running = jnp.transpose(factors)[:, 0:1] * value
        else:
            running = times(running * factors[cell : cell + 1, :], high, low)
        if cell == cells - 1:
            pair_maps[core] = running
            map_copy = remote(
                pair_maps.at[core],
                pair_maps.at[core],
                pair_send.at[0],
                pair_recv.at[0],
                partner,
            )
            map_copy.start()
        high, low = split(running)
        map_high[cell] = high
        map_low[cell] = low

    map_copy.wait()
    late_high, late_low = split(pair_maps[1])
    maps[pair] = times(pair_maps[0], late_high, late_low)
    map_copies = []
    for index, shift in enumerate(shifts):
        copy = remote(
            maps.at[pair, mine],
            maps.at[pair, mine],
            map_send.at[index],
            map_recv.at[index],
            peer(shift, 1)[0],
        )
        copy.start()
        map_copies.append(copy)

    for copy in force_copies:
        copy.wait()
    by_cell = jnp.transpose(cells_in[...], (1, 0, 2))
    for cell in range(cells):
        right = by_cell[cell]
        if cell > 0:
            right = right + factors[cell : cell + 1, :] * carried
        carried = times(right, block_high[cell], block_low[cell])
        trial[cell] = carried
    pair_states[core] = carried
    state_copy = remote(
        pair_states.at[core], pair_states.at[core], pair_send.at[1], pair_recv.at[1], partner
    )
    state_copy.start()
    state_copy.wait()
    states[pair] = times(pair_states[0], late_high, late_low) + pair_states[1]
    state_copies = []
    for index, shift in enumerate(shifts):
        copy = remote(
            states.at[pair],
            states.at[pair],
            state_send.at[index],
            state_recv.at[index],
            peer(shift, 1)[0],
        )
        copy.start()
        state_copies.append(copy)

    passed = []
    for index, shift in enumerate(shifts):
        map_copies[index].wait_recv()
        sender = peer(shift, -1)[1]
        copy = remote(
            maps.at[sender, mine],
            maps.at[sender, mine],
            pass_send.at[index],
            pass_recv.at[index],
            partner,
        )
        copy.start()
        passed.append(copy)
    for copy in passed:
        copy.wait_recv()
    for copy in state_copies:
        copy.wait_recv()

    shape = (levels, levels)
    eye = lax.broadcasted_iota(jnp.int32, shape, 0) == lax.broadcasted_iota(jnp.int32, shape, 1)
    ahead_maps[0] = jnp.where(eye, 1.0, 0.0).astype(jnp.float32)
    ahead_states[0] = jnp.zeros(ahead_states.shape[1:], jnp.float32)
    joined_map, joined_state = maps[0], states[0]
    for index in range(1, pairs):
        ahead_maps[index] = joined_map
        ahead_states[index] = joined_state
        high, low = split(maps[index])
        joined = times(jnp.concatenate([joined_map, joined_state], axis=0), high, low)
        joined_map = joined[:levels]
        joined_state = joined[levels:] + states[index]

    chain = remote(
        leaving, entering, chain_send.at[0], chain_recv.at[0], ((line + RUN) % lines_count, span)
    )

    @pl.when(first)
    def _():
        leaving[...] = joined_state
        entering[...] = jnp.zeros(entering.shape, jnp.float32)
        chain.start()

    joined_high, joined_low = split(joined_map)

    early_high, early_low = split(pair_maps[0])
    before = jnp.concatenate([ahead_maps[pair], ahead_states[pair]], axis=0)
    after = times(before, early_high, early_low)
    own_map = jnp.where(core == 1, after[:levels], before[:levels])
    own_state = jnp.where(core == 1, after[levels:] + pair_states[0], before[levels:])
    own_high, own_low = split(own_map)

    @pl.when(jnp.logical_not(first))
    def _():
        chain.wait_recv()
        leaving[...] = times(entering[...], joined_high, joined_low) + joined_state

        @pl.when(jnp.logical_not(last))
        def _():
            chain.start()

    incoming = times(entering[...], own_high, own_low) + own_state
    pieces = [
        trial[cell] + times(incoming, map_high[cell], map_low[cell]) for cell in range(cells)
    ]
    solved[...] = jnp.transpose(jnp.stack(pieces, axis=0), (1, 0, 2))

    out_copies = []
    for step in range(1, span_count):
        other = (span + step) % span_count
        other_rows = pl.ds(pl.multiple_of(other * own_lines, own_lines), own_lines)
        copy = remote(
            solved.at[other_rows],
            out.at[:, own_cells, :],
            out_send.at[step],
            out_recv.at[step],
            (line, other),
        )
        copy.start()
        out_copies.append(copy)
    keep = pltpu.make_async_copy(solved.at[own_rows], out.at[:, own_cells, :], out_sem)
    keep.start()
    for copy in map_copies + passed + state_copies:
        copy.wait_send()

    @pl.when(jnp.logical_not(last))
    def _():
        chain.wait_send()

    keep.wait()
    for copy in out_copies:
        copy.wait()


def shards(lines_count, span_count, forcing, blocks, upstream):
    own_lines, _, levels = forcing.shape
    cells = blocks.shape[0]
    lines = own_lines * span_count
    pairs = RUN * (span_count // 2)
    f32, bf16 = jnp.float32, jnp.bfloat16
    dma = pltpu.SemaphoreType.DMA
    return pl.pallas_call(
        functools.partial(kernel, lines_count, span_count),
        out_shape=jax.ShapeDtypeStruct(forcing.shape, f32),
        in_specs=[
            pl.BlockSpec(memory_space=pltpu.VMEM),
            pl.BlockSpec(memory_space=pl.ANY),
            pl.BlockSpec(memory_space=pltpu.VMEM),
        ],
        out_specs=pl.BlockSpec(memory_space=pl.ANY),
        scratch_shapes=[
            pltpu.VMEM((lines, cells, levels), f32),
            pltpu.VMEM((cells, levels, levels), f32),
            pltpu.VMEM((cells, levels, levels), bf16),
            pltpu.VMEM((cells, levels, levels), bf16),
            pltpu.VMEM((cells, levels, levels), bf16),
            pltpu.VMEM((cells, levels, levels), bf16),
            pltpu.VMEM((cells, lines, levels), f32),
            pltpu.VMEM((2, levels, levels), f32),
            pltpu.VMEM((2, lines, levels), f32),
            pltpu.VMEM((pairs, levels, levels), f32),
            pltpu.VMEM((pairs, lines, levels), f32),
            pltpu.VMEM((pairs, levels, levels), f32),
            pltpu.VMEM((pairs, lines, levels), f32),
            pltpu.VMEM((lines, levels), f32),
            pltpu.VMEM((lines, levels), f32),
            pltpu.VMEM((lines, cells, levels), f32),
            dma((cells,)),
            dma((span_count,)),
            dma((span_count,)),
            dma((2,)),
            dma((2,)),
            dma((pairs,)),
            dma((pairs,)),
            dma((pairs,)),
            dma((pairs,)),
            dma((pairs,)),
            dma((pairs,)),
            dma((1,)),
            dma((1,)),
            dma,
            dma((span_count,)),
            dma((span_count,)),
        ],
        compiler_params=pltpu.CompilerParams(
            collective_id=0, has_side_effects=True, vmem_limit_bytes=48 << 20
        ),
    )(forcing, blocks, upstream)


def solution(mesh):
    placed = (P("span", "line", None), P(("line", "span"), None, None), P(("line", "span"), None))
    return jax.shard_map(
        functools.partial(shards, mesh.shape["line"], mesh.shape["span"]),
        mesh=mesh,
        in_specs=placed,
        out_specs=P("span", "line", None),
        check_vma=False,
    )
```

```python
import functools

import jax
import jax.numpy as jnp
from jax import lax
from jax.experimental import pallas as pl
from jax.experimental.pallas import tpu as pltpu
from jax.sharding import PartitionSpec as P

MESH = pl.DeviceIdType.MESH
RUN = 2


def split(value):
    high = value.astype(jnp.bfloat16)
    return high, (value - high.astype(jnp.float32)).astype(jnp.bfloat16)


def dot(a, b):
    return jnp.dot(a, b, preferred_element_type=jnp.float32)


def times(value, high, low):
    rows = value.shape[0]
    value_high, value_low = split(value)
    both = dot(jnp.concatenate([value_high, value_low], axis=0), high)
    return both[:rows] + both[rows:] + dot(value_high, low)


def kernel(
    lines_count,
    span_count,
    forcing,
    blocks,
    upstream,
    out,
    cells_in,
    held,
    block_high,
    block_low,
    map_high,
    map_low,
    trial,
    pair_maps,
    pair_states,
    maps,
    states,
    ahead_maps,
    ahead_states,
    entering,
    leaving,
    solved,
    factors_in,
    right_high,
    right_low,
    factor_sem,
    force_sem,
    block_sem,
    force_send,
    force_recv,
    pair_send,
    pair_recv,
    map_send,
    map_recv,
    pass_send,
    pass_recv,
    state_send,
    state_recv,
    chain_send,
    chain_recv,
    out_sem,
    out_send,
    out_recv,
):
    line, span = lax.axis_index("line"), lax.axis_index("span")
    cells, levels = upstream.shape
    own_lines = forcing.shape[0]
    half_span = span_count // 2
    pairs = RUN * half_span
    runs = lines_count // RUN
    run, place = line // RUN, line % RUN
    row, core = span // 2, span % 2
    pair = place * half_span + row
    partner = (line, row * 2 + (1 - core))
    half = levels // 2
    mine = pl.ds(pl.multiple_of(core * half, half), half)

    shifts = [(a, b) for a in range(RUN) for b in range(half_span) if (a, b) != (0, 0)]

    def peer(shift, sign):
        other_place = (place + sign * shift[0] + RUN) % RUN
        other_row = (row + sign * shift[1] + half_span) % half_span
        return (run * RUN + other_place, other_row * 2 + core), other_place * half_span + other_row

    def remote(source, target, send, recv, device):
        return pltpu.make_async_remote_copy(
            src_ref=source,
            dst_ref=target,
            send_sem=send,
            recv_sem=recv,
            device_id=device,
            device_id_type=MESH,
        )

    loads = [
        pltpu.make_async_copy(blocks.at[cell], held.at[cell], block_sem.at[cell])
        for cell in range(cells)
    ]
    factor_load = pltpu.make_async_copy(upstream, factors_in, factor_sem)
    factor_load.start()
    for load in loads:
        load.start()

    barrier = pltpu.get_barrier_semaphore()
    greeted = 0
    for step in range(1, span_count):
        pl.semaphore_signal(
            barrier, inc=1, device_id=(line, (span + step) % span_count), device_id_type=MESH
        )
        greeted += 1
    for shift in shifts:
        if shift[0] != 0:
            pl.semaphore_signal(barrier, inc=1, device_id=peer(shift, 1)[0], device_id_type=MESH)
            greeted += 1
    first, last = run == 0, run == runs - 1

    @pl.when(jnp.logical_not(first))
    def _():
        pl.semaphore_signal(barrier, inc=1, device_id=(line - RUN, span), device_id_type=MESH)

    @pl.when(jnp.logical_not(last))
    def _():
        pl.semaphore_signal(barrier, inc=1, device_id=(line + RUN, span), device_id_type=MESH)

    chained = jnp.where(first, 0, 1) + jnp.where(last, 0, 1)

    own_rows = pl.ds(pl.multiple_of(span * own_lines, own_lines), own_lines)
    own_cells = pl.ds(pl.multiple_of(span * cells, cells), cells)
    stay = pltpu.make_async_copy(forcing.at[:, own_cells, :], cells_in.at[own_rows], force_sem)
    stay.start()

    force_copies = []
    factor_load.wait()
    factors = -factors_in[...]
    for cell in range(cells):
        loads[cell].wait()
        value = held[cell]
        high, low = split(value)
        block_high[cell] = high
        block_low[cell] = low
        if cell == 0:
            running = jnp.transpose(factors)[:, 0:1] * value
        else:
            running = times(running * factors[cell : cell + 1, :], high, low)
        if cell == cells - 1:
            pair_maps[core] = running
            map_copy = remote(
                pair_maps.at[core],
                pair_maps.at[core],
                pair_send.at[0],
                pair_recv.at[0],
                partner,
            )
            map_copy.start()
        high, low = split(running)
        map_high[cell] = high
        map_low[cell] = low
        if cell == min(2, cells - 2):
            pl.semaphore_wait(barrier, greeted + chained)
            for step in range(1, span_count):
                other = (span + step) % span_count
                other_cells = pl.ds(pl.multiple_of(other * cells, cells), cells)
                copy = remote(
                    forcing.at[:, other_cells, :],
                    cells_in.at[own_rows],
                    force_send.at[step],
                    force_recv.at[step],
                    (line, other),
                )
                copy.start()
                force_copies.append(copy)

    map_copy.wait()
    late_high, late_low = split(pair_maps[1])
    maps[pair] = times(pair_maps[0], late_high, late_low)
    map_copies = []
    for index, shift in enumerate(shifts):
        copy = remote(
            maps.at[pair, mine],
            maps.at[pair, mine],
            map_send.at[index],
            map_recv.at[index],
            peer(shift, 1)[0],
        )
        copy.start()
        map_copies.append(copy)

    stay.wait()
    for copy in force_copies:
        copy.wait()
    by_cell = jnp.transpose(cells_in[...], (1, 0, 2))
    for cell in range(cells):
        right = by_cell[cell]
        if cell > 0:
            right = right + factors[cell : cell + 1, :] * carried
        carried = times(right, block_high[cell], block_low[cell])
        trial[cell] = carried
    pair_states[core] = carried
    state_copy = remote(
        pair_states.at[core], pair_states.at[core], pair_send.at[1], pair_recv.at[1], partner
    )
    state_copy.start()
    state_copy.wait()
    states[pair] = times(pair_states[0], late_high, late_low) + pair_states[1]
    state_copies = []
    for index, shift in enumerate(shifts):
        copy = remote(
            states.at[pair],
            states.at[pair],
            state_send.at[index],
            state_recv.at[index],
            peer(shift, 1)[0],
        )
        copy.start()
        state_copies.append(copy)

    passed = []
    for index, shift in enumerate(shifts):
        map_copies[index].wait_recv()
        sender = peer(shift, -1)[1]
        copy = remote(
            maps.at[sender, mine],
            maps.at[sender, mine],
            pass_send.at[index],
            pass_recv.at[index],
            partner,
        )
        copy.start()
        passed.append(copy)
    for copy in passed:
        copy.wait_recv()
    for copy in state_copies:
        copy.wait_recv()

    shape = (levels, levels)
    eye = lax.broadcasted_iota(jnp.int32, shape, 0) == lax.broadcasted_iota(jnp.int32, shape, 1)
    ahead_maps[0] = jnp.where(eye, 1.0, 0.0).astype(jnp.float32)
    ahead_states[0] = jnp.zeros(ahead_states.shape[1:], jnp.float32)
    joined_state = states[0]
    for index in range(1, pairs):
        ahead_states[index] = joined_state
        high, low = split(maps[index])
        right_high[index] = high
        right_low[index] = low
        joined_state = times(joined_state, high, low) + states[index]

    chain = remote(
        leaving, entering, chain_send.at[0], chain_recv.at[0], ((line + RUN) % lines_count, span)
    )

    @pl.when(first)
    def _():
        leaving[...] = joined_state
        entering[...] = jnp.zeros(entering.shape, jnp.float32)
        chain.start()

    joined_map = maps[0]
    for index in range(1, pairs):
        ahead_maps[index] = joined_map
        joined_map = times(joined_map, right_high[index], right_low[index])
    joined_high, joined_low = split(joined_map)

    early_high, early_low = split(pair_maps[0])
    before = jnp.concatenate([ahead_maps[pair], ahead_states[pair]], axis=0)
    after = times(before, early_high, early_low)
    own_map = jnp.where(core == 1, after[:levels], before[:levels])
    own_state = jnp.where(core == 1, after[levels:] + pair_states[0], before[levels:])
    own_high, own_low = split(own_map)

    @pl.when(jnp.logical_not(first))
    def _():
        chain.wait_recv()
        leaving[...] = times(entering[...], joined_high, joined_low) + joined_state

        @pl.when(jnp.logical_not(last))
        def _():
            chain.start()

    incoming = times(entering[...], own_high, own_low) + own_state
    pieces = [
        trial[cell] + times(incoming, map_high[cell], map_low[cell]) for cell in range(cells)
    ]
    solved[...] = jnp.transpose(jnp.stack(pieces, axis=0), (1, 0, 2))

    out_copies = []
    for step in range(1, span_count):
        other = (span + step) % span_count
        other_rows = pl.ds(pl.multiple_of(other * own_lines, own_lines), own_lines)
        copy = remote(
            solved.at[other_rows],
            out.at[:, own_cells, :],
            out_send.at[step],
            out_recv.at[step],
            (line, other),
        )
        copy.start()
        out_copies.append(copy)
    keep = pltpu.make_async_copy(solved.at[own_rows], out.at[:, own_cells, :], out_sem)
    keep.start()
    for copy in map_copies + passed + state_copies:
        copy.wait_send()

    @pl.when(jnp.logical_not(last))
    def _():
        chain.wait_send()

    keep.wait()
    for copy in out_copies:
        copy.wait()


def shards(lines_count, span_count, forcing, blocks, upstream):
    own_lines, _, levels = forcing.shape
    cells = blocks.shape[0]
    lines = own_lines * span_count
    pairs = RUN * (span_count // 2)
    f32, bf16 = jnp.float32, jnp.bfloat16
    dma = pltpu.SemaphoreType.DMA
    return pl.pallas_call(
        functools.partial(kernel, lines_count, span_count),
        out_shape=jax.ShapeDtypeStruct(forcing.shape, f32),
        in_specs=[
            pl.BlockSpec(memory_space=pl.ANY),
            pl.BlockSpec(memory_space=pl.ANY),
            pl.BlockSpec(memory_space=pl.ANY),
        ],
        out_specs=pl.BlockSpec(memory_space=pl.ANY),
        scratch_shapes=[
            pltpu.VMEM((lines, cells, levels), f32),
            pltpu.VMEM((cells, levels, levels), f32),
            pltpu.VMEM((cells, levels, levels), bf16),
            pltpu.VMEM((cells, levels, levels), bf16),
            pltpu.VMEM((cells, levels, levels), bf16),
            pltpu.VMEM((cells, levels, levels), bf16),
            pltpu.VMEM((cells, lines, levels), f32),
            pltpu.VMEM((2, levels, levels), f32),
            pltpu.VMEM((2, lines, levels), f32),
            pltpu.VMEM((pairs, levels, levels), f32),
            pltpu.VMEM((pairs, lines, levels), f32),
            pltpu.VMEM((pairs, levels, levels), f32),
            pltpu.VMEM((pairs, lines, levels), f32),
            pltpu.VMEM((lines, levels), f32),
            pltpu.VMEM((lines, levels), f32),
            pltpu.VMEM((lines, cells, levels), f32),
            pltpu.VMEM((cells, levels), f32),
            pltpu.VMEM((pairs, levels, levels), bf16),
            pltpu.VMEM((pairs, levels, levels), bf16),
            dma,
            dma,
            dma((cells,)),
            dma((span_count,)),
            dma((span_count,)),
            dma((2,)),
            dma((2,)),
            dma((pairs,)),
            dma((pairs,)),
            dma((pairs,)),
            dma((pairs,)),
            dma((pairs,)),
            dma((pairs,)),
            dma((1,)),
            dma((1,)),
            dma,
            dma((span_count,)),
            dma((span_count,)),
        ],
        compiler_params=pltpu.CompilerParams(
            collective_id=0, has_side_effects=True, vmem_limit_bytes=67043328
        ),
    )(forcing, blocks, upstream)


def solution(mesh):
    placed = (P("span", "line", None), P(("line", "span"), None, None), P(("line", "span"), None))
    return jax.shard_map(
        functools.partial(shards, mesh.shape["line"], mesh.shape["span"]),
        mesh=mesh,
        in_specs=placed,
        out_specs=P("span", "line", None),
        check_vma=False,
    )
```

```python
import functools

import jax
import jax.numpy as jnp
from jax import lax
from jax.experimental import pallas as pl
from jax.experimental.pallas import tpu as pltpu
from jax.sharding import PartitionSpec as P

MESH = pl.DeviceIdType.MESH
RUN = 2


def split(value):
    high = value.astype(jnp.bfloat16)
    return high, (value - high.astype(jnp.float32)).astype(jnp.bfloat16)


def dot(a, b):
    return jnp.dot(a, b, preferred_element_type=jnp.float32)


def times(value, high, low):
    rows = value.shape[0]
    value_high, value_low = split(value)
    both = dot(jnp.concatenate([value_high, value_low], axis=0), high)
    return both[:rows] + both[rows:] + dot(value_high, low)


def kernel(
    lines_count,
    span_count,
    forcing,
    blocks,
    upstream,
    out,
    cells_in,
    held,
    block_high,
    block_low,
    map_high,
    map_low,
    trial,
    pair_maps,
    pair_states,
    maps,
    states,
    ahead_maps,
    ahead_states,
    entering,
    leaving,
    solved,
    factors_in,
    right_high,
    right_low,
    factor_sem,
    force_sem,
    block_sem,
    force_send,
    force_recv,
    pair_send,
    pair_recv,
    map_send,
    map_recv,
    pass_send,
    pass_recv,
    state_send,
    state_recv,
    chain_send,
    chain_recv,
    out_sem,
    out_send,
    out_recv,
):
    line, span = lax.axis_index("line"), lax.axis_index("span")
    cells, levels = upstream.shape
    own_lines = forcing.shape[0]
    half_span = span_count // 2
    pairs = RUN * half_span
    runs = lines_count // RUN
    run, place = line // RUN, line % RUN
    row, core = span // 2, span % 2
    pair = place * half_span + row
    partner = (line, row * 2 + (1 - core))
    half = levels // 2
    mine = pl.ds(pl.multiple_of(core * half, half), half)

    shifts = [(a, b) for a in range(RUN) for b in range(half_span) if (a, b) != (0, 0)]

    def peer(shift, sign):
        other_place = (place + sign * shift[0] + RUN) % RUN
        other_row = (row + sign * shift[1] + half_span) % half_span
        return (run * RUN + other_place, other_row * 2 + core), other_place * half_span + other_row

    def remote(source, target, send, recv, device):
        return pltpu.make_async_remote_copy(
            src_ref=source,
            dst_ref=target,
            send_sem=send,
            recv_sem=recv,
            device_id=device,
            device_id_type=MESH,
        )

    loads = [
        pltpu.make_async_copy(blocks.at[cell], held.at[cell], block_sem.at[cell])
        for cell in range(cells)
    ]
    factor_load = pltpu.make_async_copy(upstream, factors_in, factor_sem)
    factor_load.start()
    for load in loads:
        load.start()

    barrier = pltpu.get_barrier_semaphore()
    greeted = 0
    for step in range(1, span_count):
        pl.semaphore_signal(
            barrier, inc=1, device_id=(line, (span + step) % span_count), device_id_type=MESH
        )
        greeted += 1
    for shift in shifts:
        if shift[0] != 0:
            pl.semaphore_signal(barrier, inc=1, device_id=peer(shift, 1)[0], device_id_type=MESH)
            greeted += 1
    first, last = run == 0, run == runs - 1

    @pl.when(jnp.logical_not(first))
    def _():
        pl.semaphore_signal(barrier, inc=1, device_id=(line - RUN, span), device_id_type=MESH)

    @pl.when(jnp.logical_not(last))
    def _():
        pl.semaphore_signal(barrier, inc=1, device_id=(line + RUN, span), device_id_type=MESH)

    chained = jnp.where(first, 0, 1) + jnp.where(last, 0, 1)

    own_rows = pl.ds(pl.multiple_of(span * own_lines, own_lines), own_lines)
    own_cells = pl.ds(pl.multiple_of(span * cells, cells), cells)
    stay = pltpu.make_async_copy(forcing.at[:, own_cells, :], cells_in.at[own_rows], force_sem)
    stay.start()

    force_copies = []
    factor_load.wait()
    factors = -factors_in[...]
    for cell in range(cells):
        loads[cell].wait()
        value = held[cell]
        high, low = split(value)
        block_high[cell] = high
        block_low[cell] = low
        if cell == 0:
            running = jnp.transpose(factors)[:, 0:1] * value
        else:
            running = times(running * factors[cell : cell + 1, :], high, low)
        if cell == cells - 1:
            pair_maps[core] = running
            map_copy = remote(
                pair_maps.at[core],
                pair_maps.at[core],
                pair_send.at[0],
                pair_recv.at[0],
                partner,
            )
            map_copy.start()
        high, low = split(running)
        map_high[cell] = high
        map_low[cell] = low
        if cell == min(2, cells - 2):
            pl.semaphore_wait(barrier, greeted + chained)
            for step in range(1, span_count):
                other = (span + step) % span_count
                other_cells = pl.ds(pl.multiple_of(other * cells, cells), cells)
                copy = remote(
                    forcing.at[:, other_cells, :],
                    cells_in.at[own_rows],
                    force_send.at[step],
                    force_recv.at[step],
                    (line, other),
                )
                copy.start()
                force_copies.append(copy)

    map_copy.wait()
    late_high, late_low = split(pair_maps[1])
    maps[pair] = times(pair_maps[0], late_high, late_low)
    map_copies = []
    for index, shift in enumerate(shifts):
        copy = remote(
            maps.at[pair, mine],
            maps.at[pair, mine],
            map_send.at[index],
            map_recv.at[index],
            peer(shift, 1)[0],
        )
        copy.start()
        map_copies.append(copy)

    stay.wait()
    for copy in force_copies:
        copy.wait()
    by_cell = jnp.transpose(cells_in[...], (1, 0, 2))
    for cell in range(cells):
        right = by_cell[cell]
        if cell > 0:
            right = right + factors[cell : cell + 1, :] * carried
        carried = times(right, block_high[cell], block_low[cell])
        trial[cell] = carried
    pair_states[core] = carried
    state_copy = remote(
        pair_states.at[core], pair_states.at[core], pair_send.at[1], pair_recv.at[1], partner
    )
    state_copy.start()
    state_copy.wait()
    states[pair] = times(pair_states[0], late_high, late_low) + pair_states[1]
    state_copies = []
    for index, shift in enumerate(shifts):
        copy = remote(
            states.at[pair],
            states.at[pair],
            state_send.at[index],
            state_recv.at[index],
            peer(shift, 1)[0],
        )
        copy.start()
        state_copies.append(copy)

    passed = []
    for index, shift in enumerate(shifts):
        map_copies[index].wait_recv()
        sender = peer(shift, -1)[1]
        copy = remote(
            maps.at[sender, mine],
            maps.at[sender, mine],
            pass_send.at[index],
            pass_recv.at[index],
            partner,
        )
        copy.start()
        passed.append(copy)
    for copy in passed:
        copy.wait_recv()
    for copy in state_copies:
        copy.wait_recv()

    shape = (levels, levels)
    eye = lax.broadcasted_iota(jnp.int32, shape, 0) == lax.broadcasted_iota(jnp.int32, shape, 1)
    ahead_maps[0] = jnp.where(eye, 1.0, 0.0).astype(jnp.float32)
    ahead_states[0] = jnp.zeros(ahead_states.shape[1:], jnp.float32)
    joined_state = states[0]
    for index in range(1, pairs):
        ahead_states[index] = joined_state
        high, low = split(maps[index])
        right_high[index] = high
        right_low[index] = low
        joined_state = times(joined_state, high, low) + states[index]

    chain = remote(
        leaving, entering, chain_send.at[0], chain_recv.at[0], ((line + RUN) % lines_count, span)
    )

    @pl.when(first)
    def _():
        leaving[...] = joined_state
        entering[...] = jnp.zeros(entering.shape, jnp.float32)
        chain.start()

    joined_map = maps[0]
    for index in range(1, pairs):
        ahead_maps[index] = joined_map
        joined_map = times(joined_map, right_high[index], right_low[index])
    joined_high, joined_low = split(joined_map)

    early_high, early_low = split(pair_maps[0])
    before = jnp.concatenate([ahead_maps[pair], ahead_states[pair]], axis=0)
    after = times(before, early_high, early_low)
    own_map = jnp.where(core == 1, after[:levels], before[:levels])
    own_state = jnp.where(core == 1, after[levels:] + pair_states[0], before[levels:])
    own_high, own_low = split(own_map)

    @pl.when(jnp.logical_not(first))
    def _():
        chain.wait_recv()
        leaving[...] = times(entering[...], joined_high, joined_low) + joined_state

        @pl.when(jnp.logical_not(last))
        def _():
            chain.start()

    incoming = times(entering[...], own_high, own_low) + own_state
    pieces = [
        trial[cell] + times(incoming, map_high[cell], map_low[cell]) for cell in range(cells)
    ]
    solved[...] = jnp.transpose(jnp.stack(pieces, axis=0), (1, 0, 2))

    out_copies = []
    for step in range(1, span_count):
        other = (span + step) % span_count
        other_rows = pl.ds(pl.multiple_of(other * own_lines, own_lines), own_lines)
        copy = remote(
            solved.at[other_rows],
            out.at[:, own_cells, :],
            out_send.at[step],
            out_recv.at[step],
            (line, other),
        )
        copy.start()
        out_copies.append(copy)
    keep = pltpu.make_async_copy(solved.at[own_rows], out.at[:, own_cells, :], out_sem)
    keep.start()
    for copy in map_copies + passed + state_copies:
        copy.wait_send()

    @pl.when(jnp.logical_not(last))
    def _():
        chain.wait_send()

    keep.wait()
    for copy in out_copies:
        copy.wait()


def shards(lines_count, span_count, forcing, blocks, upstream):
    own_lines, _, levels = forcing.shape
    cells = blocks.shape[0]
    lines = own_lines * span_count
    pairs = RUN * (span_count // 2)
    f32, bf16 = jnp.float32, jnp.bfloat16
    dma = pltpu.SemaphoreType.DMA
    return pl.pallas_call(
        functools.partial(kernel, lines_count, span_count),
        out_shape=jax.ShapeDtypeStruct(forcing.shape, f32),
        in_specs=[
            pl.BlockSpec(memory_space=pl.ANY),
            pl.BlockSpec(memory_space=pl.ANY),
            pl.BlockSpec(memory_space=pl.ANY),
        ],
        out_specs=pl.BlockSpec(memory_space=pl.ANY),
        scratch_shapes=[
            pltpu.VMEM((lines, cells, levels), f32),
            pltpu.VMEM((cells, levels, levels), f32),
            pltpu.VMEM((cells, levels, levels), bf16),
            pltpu.VMEM((cells, levels, levels), bf16),
            pltpu.VMEM((cells, levels, levels), bf16),
            pltpu.VMEM((cells, levels, levels), bf16),
            pltpu.VMEM((cells, lines, levels), f32),
            pltpu.VMEM((2, levels, levels), f32),
            pltpu.VMEM((2, lines, levels), f32),
            pltpu.VMEM((pairs, levels, levels), f32),
            pltpu.VMEM((pairs, lines, levels), f32),
            pltpu.VMEM((pairs, levels, levels), f32),
            pltpu.VMEM((pairs, lines, levels), f32),
            pltpu.VMEM((lines, levels), f32),
            pltpu.VMEM((lines, levels), f32),
            pltpu.VMEM((lines, cells, levels), f32),
            pltpu.VMEM((cells, levels), f32),
            pltpu.VMEM((pairs, levels, levels), bf16),
            pltpu.VMEM((pairs, levels, levels), bf16),
            dma,
            dma,
            dma((cells,)),
            dma((span_count,)),
            dma((span_count,)),
            dma((2,)),
            dma((2,)),
            dma((pairs,)),
            dma((pairs,)),
            dma((pairs,)),
            dma((pairs,)),
            dma((pairs,)),
            dma((pairs,)),
            dma((1,)),
            dma((1,)),
            dma,
            dma((span_count,)),
            dma((span_count,)),
        ],
        compiler_params=pltpu.CompilerParams(
            collective_id=0, has_side_effects=True, vmem_limit_bytes=48 << 20
        ),
    )(*[pltpu.with_memory_space_constraint(x, pltpu.MemorySpace.HBM) for x in (forcing, blocks, upstream)])


def solution(mesh):
    placed = (P("span", "line", None), P(("line", "span"), None, None), P(("line", "span"), None))
    return jax.shard_map(
        functools.partial(shards, mesh.shape["line"], mesh.shape["span"]),
        mesh=mesh,
        in_specs=placed,
        out_specs=P("span", "line", None),
        check_vma=False,
    )
```

```python
import functools

import jax
import jax.numpy as jnp
from jax import lax
from jax.experimental import pallas as pl
from jax.experimental.pallas import tpu as pltpu
from jax.sharding import PartitionSpec as P

MESH = pl.DeviceIdType.MESH
RUN = 2


def split(value):
    high = value.astype(jnp.bfloat16)
    return high, (value - high.astype(jnp.float32)).astype(jnp.bfloat16)


def dot(a, b):
    return jnp.dot(a, b, preferred_element_type=jnp.float32)


def times(value, high, low):
    rows = value.shape[0]
    value_high, value_low = split(value)
    both = dot(jnp.concatenate([value_high, value_low], axis=0), high)
    return both[:rows] + both[rows:] + dot(value_high, low)


def kernel(
    lines_count,
    span_count,
    forcing,
    blocks,
    upstream,
    out,
    cells_in,
    held,
    block_high,
    block_low,
    map_high,
    map_low,
    trial,
    pair_maps,
    pair_states,
    maps,
    states,
    ahead_maps,
    ahead_states,
    entering,
    leaving,
    solved,
    factors_in,
    right_high,
    right_low,
    factor_sem,
    force_sem,
    block_sem,
    force_send,
    force_recv,
    pair_send,
    pair_recv,
    map_send,
    map_recv,
    pass_send,
    pass_recv,
    state_send,
    state_recv,
    chain_send,
    chain_recv,
    out_sem,
    out_send,
    out_recv,
):
    line, span = lax.axis_index("line"), lax.axis_index("span")
    cells, levels = upstream.shape
    own_lines = forcing.shape[0]
    half_span = span_count // 2
    pairs = RUN * half_span
    runs = lines_count // RUN
    run, place = line // RUN, line % RUN
    row, core = span // 2, span % 2
    pair = place * half_span + row
    partner = (line, row * 2 + (1 - core))
    half = levels // 2
    mine = pl.ds(pl.multiple_of(core * half, half), half)

    shifts = [(a, b) for a in range(RUN) for b in range(half_span) if (a, b) != (0, 0)]
    shifts.sort(key=lambda shift: (shift[0] == 0) + (shift[1] == 0))

    def peer(shift, sign):
        other_place = (place + sign * shift[0] + RUN) % RUN
        other_row = (row + sign * shift[1] + half_span) % half_span
        return (run * RUN + other_place, other_row * 2 + core), other_place * half_span + other_row

    def remote(source, target, send, recv, device):
        return pltpu.make_async_remote_copy(
            src_ref=source,
            dst_ref=target,
            send_sem=send,
            recv_sem=recv,
            device_id=device,
            device_id_type=MESH,
        )

    loads = [
        pltpu.make_async_copy(blocks.at[cell], held.at[cell], block_sem.at[cell])
        for cell in range(cells)
    ]
    factor_load = pltpu.make_async_copy(upstream, factors_in, factor_sem)
    factor_load.start()
    for load in loads:
        load.start()

    barrier = pltpu.get_barrier_semaphore()
    greeted = 0
    for step in range(1, span_count):
        pl.semaphore_signal(
            barrier, inc=1, device_id=(line, (span + step) % span_count), device_id_type=MESH
        )
        greeted += 1
    for shift in shifts:
        if shift[0] != 0:
            pl.semaphore_signal(barrier, inc=1, device_id=peer(shift, 1)[0], device_id_type=MESH)
            greeted += 1
    first, last = run == 0, run == runs - 1

    @pl.when(jnp.logical_not(first))
    def _():
        pl.semaphore_signal(barrier, inc=1, device_id=(line - RUN, span), device_id_type=MESH)

    @pl.when(jnp.logical_not(last))
    def _():
        pl.semaphore_signal(barrier, inc=1, device_id=(line + RUN, span), device_id_type=MESH)

    chained = jnp.where(first, 0, 1) + jnp.where(last, 0, 1)

    own_rows = pl.ds(pl.multiple_of(span * own_lines, own_lines), own_lines)
    own_cells = pl.ds(pl.multiple_of(span * cells, cells), cells)
    stay = pltpu.make_async_copy(forcing.at[:, own_cells, :], cells_in.at[own_rows], force_sem)
    stay.start()

    force_copies = []
    factor_load.wait()
    factors = -factors_in[...]
    for cell in range(cells):
        loads[cell].wait()
        value = held[cell]
        high, low = split(value)
        block_high[cell] = high
        block_low[cell] = low
        if cell == 0:
            running = jnp.transpose(factors)[:, 0:1] * value
        else:
            running = times(running * factors[cell : cell + 1, :], high, low)
        if cell == cells - 1:
            pair_maps[core] = running
            map_copy = remote(
                pair_maps.at[core],
                pair_maps.at[core],
                pair_send.at[0],
                pair_recv.at[0],
                partner,
            )
            map_copy.start()
        high, low = split(running)
        map_high[cell] = high
        map_low[cell] = low
        if cell == min(2, cells - 2):
            pl.semaphore_wait(barrier, greeted + chained)
            for step in range(1, span_count):
                other = (span + step) % span_count
                other_cells = pl.ds(pl.multiple_of(other * cells, cells), cells)
                copy = remote(
                    forcing.at[:, other_cells, :],
                    cells_in.at[own_rows],
                    force_send.at[step],
                    force_recv.at[step],
                    (line, other),
                )
                copy.start()
                force_copies.append(copy)

    map_copy.wait()
    late_high, late_low = split(pair_maps[1])
    maps[pair] = times(pair_maps[0], late_high, late_low)
    map_copies = []
    for index, shift in enumerate(shifts):
        copy = remote(
            maps.at[pair, mine],
            maps.at[pair, mine],
            map_send.at[index],
            map_recv.at[index],
            peer(shift, 1)[0],
        )
        copy.start()
        map_copies.append(copy)

    stay.wait()
    for copy in force_copies:
        copy.wait()
    by_cell = jnp.transpose(cells_in[...], (1, 0, 2))
    for cell in range(cells):
        right = by_cell[cell]
        if cell > 0:
            right = right + factors[cell : cell + 1, :] * carried
        carried = times(right, block_high[cell], block_low[cell])
        trial[cell] = carried
    pair_states[core] = carried
    state_copy = remote(
        pair_states.at[core], pair_states.at[core], pair_send.at[1], pair_recv.at[1], partner
    )
    state_copy.start()
    state_copy.wait()
    states[pair] = times(pair_states[0], late_high, late_low) + pair_states[1]
    state_copies = []
    for index, shift in enumerate(shifts):
        copy = remote(
            states.at[pair],
            states.at[pair],
            state_send.at[index],
            state_recv.at[index],
            peer(shift, 1)[0],
        )
        copy.start()
        state_copies.append(copy)

    passed = []
    for index, shift in enumerate(shifts):
        map_copies[index].wait_recv()
        sender = peer(shift, -1)[1]
        copy = remote(
            maps.at[sender, mine],
            maps.at[sender, mine],
            pass_send.at[index],
            pass_recv.at[index],
            partner,
        )
        copy.start()
        passed.append(copy)
    for copy in passed:
        copy.wait_recv()
    for copy in state_copies:
        copy.wait_recv()

    shape = (levels, levels)
    eye = lax.broadcasted_iota(jnp.int32, shape, 0) == lax.broadcasted_iota(jnp.int32, shape, 1)
    ahead_maps[0] = jnp.where(eye, 1.0, 0.0).astype(jnp.float32)
    ahead_states[0] = jnp.zeros(ahead_states.shape[1:], jnp.float32)
    joined_state = states[0]
    for index in range(1, pairs):
        ahead_states[index] = joined_state
        high, low = split(maps[index])
        right_high[index] = high
        right_low[index] = low
        joined_state = times(joined_state, high, low) + states[index]

    chain = remote(
        leaving, entering, chain_send.at[0], chain_recv.at[0], ((line + RUN) % lines_count, span)
    )

    @pl.when(first)
    def _():
        leaving[...] = joined_state
        entering[...] = jnp.zeros(entering.shape, jnp.float32)
        chain.start()

    joined_map = maps[0]
    for index in range(1, pairs):
        ahead_maps[index] = joined_map
        joined_map = times(joined_map, right_high[index], right_low[index])
    joined_high, joined_low = split(joined_map)

    early_high, early_low = split(pair_maps[0])
    before = jnp.concatenate([ahead_maps[pair], ahead_states[pair]], axis=0)
    after = times(before, early_high, early_low)
    own_map = jnp.where(core == 1, after[:levels], before[:levels])
    own_state = jnp.where(core == 1, after[levels:] + pair_states[0], before[levels:])
    own_high, own_low = split(own_map)

    @pl.when(jnp.logical_not(first))
    def _():
        chain.wait_recv()
        leaving[...] = times(entering[...], joined_high, joined_low) + joined_state

        @pl.when(jnp.logical_not(last))
        def _():
            chain.start()

    incoming = times(entering[...], own_high, own_low) + own_state
    pieces = [
        trial[cell] + times(incoming, map_high[cell], map_low[cell]) for cell in range(cells)
    ]
    solved[...] = jnp.transpose(jnp.stack(pieces, axis=0), (1, 0, 2))

    out_copies = []
    for step in range(1, span_count):
        other = (span + step) % span_count
        other_rows = pl.ds(pl.multiple_of(other * own_lines, own_lines), own_lines)
        copy = remote(
            solved.at[other_rows],
            out.at[:, own_cells, :],
            out_send.at[step],
            out_recv.at[step],
            (line, other),
        )
        copy.start()
        out_copies.append(copy)
    keep = pltpu.make_async_copy(solved.at[own_rows], out.at[:, own_cells, :], out_sem)
    keep.start()
    for copy in map_copies + passed + state_copies:
        copy.wait_send()

    @pl.when(jnp.logical_not(last))
    def _():
        chain.wait_send()

    keep.wait()
    for copy in out_copies:
        copy.wait()


def shards(lines_count, span_count, forcing, blocks, upstream):
    own_lines, _, levels = forcing.shape
    cells = blocks.shape[0]
    lines = own_lines * span_count
    pairs = RUN * (span_count // 2)
    f32, bf16 = jnp.float32, jnp.bfloat16
    dma = pltpu.SemaphoreType.DMA
    return pl.pallas_call(
        functools.partial(kernel, lines_count, span_count),
        out_shape=jax.ShapeDtypeStruct(forcing.shape, f32),
        in_specs=[
            pl.BlockSpec(memory_space=pl.ANY),
            pl.BlockSpec(memory_space=pl.ANY),
            pl.BlockSpec(memory_space=pl.ANY),
        ],
        out_specs=pl.BlockSpec(memory_space=pl.ANY),
        scratch_shapes=[
            pltpu.VMEM((lines, cells, levels), f32),
            pltpu.VMEM((cells, levels, levels), f32),
            pltpu.VMEM((cells, levels, levels), bf16),
            pltpu.VMEM((cells, levels, levels), bf16),
            pltpu.VMEM((cells, levels, levels), bf16),
            pltpu.VMEM((cells, levels, levels), bf16),
            pltpu.VMEM((cells, lines, levels), f32),
            pltpu.VMEM((2, levels, levels), f32),
            pltpu.VMEM((2, lines, levels), f32),
            pltpu.VMEM((pairs, levels, levels), f32),
            pltpu.VMEM((pairs, lines, levels), f32),
            pltpu.VMEM((pairs, levels, levels), f32),
            pltpu.VMEM((pairs, lines, levels), f32),
            pltpu.VMEM((lines, levels), f32),
            pltpu.VMEM((lines, levels), f32),
            pltpu.VMEM((lines, cells, levels), f32),
            pltpu.VMEM((cells, levels), f32),
            pltpu.VMEM((pairs, levels, levels), bf16),
            pltpu.VMEM((pairs, levels, levels), bf16),
            dma,
            dma,
            dma((cells,)),
            dma((span_count,)),
            dma((span_count,)),
            dma((2,)),
            dma((2,)),
            dma((pairs,)),
            dma((pairs,)),
            dma((pairs,)),
            dma((pairs,)),
            dma((pairs,)),
            dma((pairs,)),
            dma((1,)),
            dma((1,)),
            dma,
            dma((span_count,)),
            dma((span_count,)),
        ],
        compiler_params=pltpu.CompilerParams(
            collective_id=0, has_side_effects=True, vmem_limit_bytes=48 << 20
        ),
    )(*[pltpu.with_memory_space_constraint(x, pltpu.MemorySpace.HBM) for x in (forcing, blocks, upstream)])


def solution(mesh):
    placed = (P("span", "line", None), P(("line", "span"), None, None), P(("line", "span"), None))
    return jax.shard_map(
        functools.partial(shards, mesh.shape["line"], mesh.shape["span"]),
        mesh=mesh,
        in_specs=placed,
        out_specs=P("span", "line", None),
        check_vma=False,
    )
```
